32 devices in a mesh: mp: 2 (over x), width: 2 (over y), hidden: 8 (over z, core).
Axes of the slice: x: 2, y: 2, z: 4, core: 2. Of those that a mesh axis runs over, the one named last changes fastest.
Arguments:
- residual_in: bfloat16 [2, 512, 3584], P('mp', 'hidden'), may hold values from -6 to 6
- gate_weight: bfloat16 [2, 14336, 3584], P('mp', ('width', 'hidden')), may hold values from -0.09375 to 0.09375
- up_weight: bfloat16 [2, 14336, 3584], P('mp', ('width', 'hidden')), may hold values from -0.09375 to 0.09375
- down_weight: bfloat16 [2, 14336, 3584], P('mp', ('width', 'hidden')), may hold values from -0.046875 to 0.046875
- enc_weight: float32 [7168, 16384], P(('mp', 'width'), 'hidden'), may hold values from -0.0625 to 0.0625
- enc_bias: float32 [16384], P('hidden'), may hold values from -3 to 3
- dec_weight: float32 [16384, 7168], P('hidden', ('mp', 'width')), may hold values from -0.25 to 0.25
- dec_bias: float32 [7168], P(('mp', 'width')), may hold values from -2 to 2
Outputs:
- mlp_acts: bfloat16 [2, 512, 3584], P('mp', 'hidden', 'width')
- latents: float32 [512, 16384], P(None, 'hidden')
- grad_enc: float32 [7168, 16384], P(('mp', 'width'), 'hidden')
- grad_dec: float32 [16384, 7168], P('hidden', ('mp', 'width'))
- grad_enc_bias: float32 [16384], P('hidden')
- grad_dec_bias: float32 [7168], P(('mp', 'width'))
The draws below stay inside these ranges and needn't reach their ends.
All inputs are finite; a program needn't handle non-finite values.
Results may differ from the reference program's by a relative error of at most 0.0058.
Values may be sent and summed in bfloat16 or wider, within the bound.
A program may use at most 192 MiB of HBM per device.

```python
import math
import jax
import jax.numpy as jnp
from jax import lax

D = 3584
FF = 14336
LATENTS = 16384
TOKENS = 512
CODER = 7168


def draw_dec_weight(key, part):
    base_key, row_key, col_key = jax.random.split(key, 3)
    base = jnp.clip(jax.random.normal(base_key, (LATENTS, 2 * D), jnp.float32), -4.0, 4.0)
    top_log = math.log(10.0)
    row_scale = jnp.exp(jax.random.uniform(row_key, (LATENTS, 1), jnp.float32, 0.0, top_log))
    col_scale = jnp.exp(jax.random.uniform(col_key, (1, 2 * D), jnp.float32, 0.0, top_log))
    drawn = base * row_scale * col_scale / (16.0 * math.sqrt(LATENTS))
    return jnp.clip(drawn, -0.25, 0.25)


def shard_levels(stream_key, shape, cuts, low, high):
    def one(position, parts):
        draws = jax.random.uniform(jax.random.fold_in(jax.random.fold_in(stream_key, 6), position), (parts,), jnp.float32, low / len(cuts), high / len(cuts))
        return jnp.repeat(jnp.exp(draws), shape[position] // parts).reshape((-1,) + (1,) * (len(shape) - position - 1))

    level = one(*cuts[0])
    for cut in cuts[1:]:
        level = level * one(*cut)
    return level


def noise(key, shape, scale, limit, cuts=(), kind=jnp.bfloat16):
    gain = shard_levels(key, shape, cuts, -0.22, 0.18) if cuts else 1.0
    values = jax.random.normal(key, shape, jnp.float32) * scale * gain
    return jnp.minimum(jnp.maximum(values, -limit), limit).astype(kind)


def setup_inputs(seed: int = 0) -> dict:
    key_of = jax.random.split(jax.random.key(seed), 9)
    residual_in = noise(key_of[0], (2, TOKENS, D), 1.0, 6.0, ((0, 2), (1, 8)))
    gate_weight = noise(key_of[1], (2, FF, D), D ** -0.5, 0.09375, ((0, 2), (1, 16)))
    up_weight = noise(key_of[2], (2, FF, D), D ** -0.5, 0.09375, ((0, 2), (1, 16)))
    down_weight = noise(key_of[3], (2, FF, D), FF ** -0.5, 0.046875, ((0, 2), (1, 16)))
    enc_weight = noise(key_of[4], (CODER, LATENTS), CODER ** -0.5, 0.0625, ((0, 4), (1, 8)), jnp.float32)
    enc_bias = noise(key_of[5], (LATENTS,), 0.5, 3.0, ((0, 8),), jnp.float32)
    dec_weight = draw_dec_weight(jax.random.fold_in(key_of[8], 71), 0)
    dec_bias = noise(key_of[7], (CODER,), 0.3, 2.0, ((0, 4),), jnp.float32)
    return dict(residual_in=residual_in, gate_weight=gate_weight, up_weight=up_weight, down_weight=down_weight, enc_weight=enc_weight, enc_bias=enc_bias, dec_weight=dec_weight, dec_bias=dec_bias)


sharpness = 8.0
sparsity_coef = 0.02
norm_floor = 1e-06
highest = lax.Precision.HIGHEST

def reference(residual_in, gate_weight, up_weight, down_weight, enc_weight, enc_bias, dec_weight, dec_bias):
    last_last = (((1,), (1,)), ((), ()))
    first_first = (((0,), (0,)), ((), ()))
    outputs = []
    for model_idx in range(2):
        gate_act = lax.dot_general(residual_in[model_idx], gate_weight[model_idx], last_last, preferred_element_type=jnp.float32)
        up_act = lax.dot_general(residual_in[model_idx], up_weight[model_idx], last_last, preferred_element_type=jnp.float32)
        hidden_act = (jax.nn.gelu(gate_act, approximate=True) * up_act).astype(jnp.bfloat16)
        model_out = jnp.dot(hidden_act, down_weight[model_idx], preferred_element_type=jnp.float32)
        outputs.append(model_out.astype(jnp.bfloat16))
    mlp_acts = jnp.stack(outputs)
    coder_in = jnp.concatenate(outputs, axis=1).astype(jnp.float32)
    pre_act = jnp.dot(coder_in, enc_weight, precision=highest) + enc_bias
    latents = jax.nn.softplus(sharpness * pre_act) / sharpness
    first_part = dec_weight[:, :D]
    second_part = dec_weight[:, D:]
    first_norm = jnp.sqrt(lax.optimization_barrier(jnp.sum(first_part * first_part, axis=1)) + norm_floor)
    second_norm = jnp.sqrt(lax.optimization_barrier(jnp.sum(second_part * second_part, axis=1)) + norm_floor)
    rebuilt = jnp.dot(latents, dec_weight, precision=highest) + dec_bias
    err_grad = 2.0 / TOKENS * (rebuilt - coder_in)
    grad_dec_bias = lax.optimization_barrier(jnp.sum(err_grad, axis=0))
    lat_grad = lax.dot_general(err_grad, dec_weight, last_last, precision=highest, preferred_element_type=jnp.float32)
    lat_grad = lat_grad + sparsity_coef * (first_norm + second_norm)
    pre_grad = lat_grad * jax.nn.sigmoid(sharpness * pre_act)
    grad_enc_bias = lax.optimization_barrier(jnp.sum(pre_grad, axis=0))
    grad_enc = lax.dot_general(coder_in, pre_grad, first_first, precision=highest, preferred_element_type=jnp.float32)
    latent_totals = lax.optimization_barrier(jnp.sum(latents, axis=0))
    penalty_part = jnp.concatenate([first_part * (latent_totals / first_norm)[:, None], second_part * (latent_totals / second_norm)[:, None]], axis=1)
    grad_dec = lax.dot_general(latents, err_grad, first_first, precision=highest, preferred_element_type=jnp.float32) + sparsity_coef * penalty_part
    return (mlp_acts, latents, grad_enc, grad_dec, grad_enc_bias, grad_dec_bias)
```

```python
import jax
import jax.numpy as jnp
from jax import lax
from jax.sharding import PartitionSpec as P

sharpness = 8.0
sparsity_coef = 0.02
norm_floor = 1e-06
bf16 = jnp.bfloat16
f32 = jnp.float32
CHUNKS = 2
CORE_TYPE = f32


def swap(value, axis):
    return lax.ppermute(value, axis, [(0, 1), (1, 0)])


def partner(value, offset, size):
    return lax.ppermute(value, "hidden", [(i, i ^ offset) for i in range(size)])


def keep_bf16(value):
    return lax.reduce_precision(value, 8, 7).astype(bf16)


def after(value, earlier):
    return lax.optimization_barrier((value, earlier))[0]


def gather_hidden(own, size):
    mine = jnp.stack([own] + [partner(own, 2 * d, size) for d in range(1, size // 2)])
    return jnp.stack([mine, partner(mine, 1, size)])


def scatter_hidden_chip(part, size):
    return part[0] + partner(part[1].astype(CORE_TYPE), 1, size).astype(f32)


def scatter_hidden_z(part, size):
    total = part[0]
    for d in range(1, size // 2):
        total = total + partner(part[d].astype(bf16), 2 * d, size).astype(f32)
    return total


def half(value, index):
    rows = value.shape[0] // 2
    return lax.dynamic_slice_in_dim(value, index * rows, rows, 0)


def join(mine, other, index):
    first = jnp.where(index == 0, mine, other)
    second = jnp.where(index == 0, other, mine)
    return jnp.concatenate([first, second], axis=0)


def sum_pair(value, first, second):
    i, j = lax.axis_index(first), lax.axis_index(second)
    once = half(value, i) + swap(half(value, 1 - i).astype(bf16), first).astype(f32)
    twice = half(once, j) + swap(half(once, 1 - j).astype(bf16), second).astype(f32)
    own = keep_bf16(twice)
    pair = join(own, swap(own, second), j)
    return join(pair, swap(pair, first), i)


def sum_models(value):
    rows = value.shape[0] // 2
    return jnp.concatenate(
        [sum_pair(value[:rows], "mp", "width"), sum_pair(value[rows:], "width", "mp")], axis=0
    )


def body(
    size,
    residual_in,
    gate_weight,
    up_weight,
    down_weight,
    enc_weight,
    enc_bias,
    dec_weight,
    dec_bias,
):
    last_last = (((1,), (1,)), ((), ()))
    first_first = (((0,), (0,)), ((), ()))
    tokens = residual_in.shape[1] * size
    mine, width, features = residual_in.shape[1] // CHUNKS, lax.axis_index("width"), residual_in.shape[2]
    model_index = lax.axis_index("mp")
    rows = mine * size
    halves = features // 2
    enc = enc_weight.astype(bf16)
    dec = dec_weight.astype(bf16)
    squares = jnp.sum(dec_weight * dec_weight, axis=1)

    def dot(a, b, dims):
        return lax.dot_general(a, b, dims, preferred_element_type=f32)

    plain = (((1,), (0,)), ((), ()))

    def gather_half(own):
        part = lax.dynamic_slice_in_dim(own, width * halves, halves, 1)
        return jnp.stack([partner(part, 2 * d, size) for d in range(1, size // 2)])

    def gather_residual(own, far):
        other = swap(far, "width")
        far = jnp.concatenate(
            [jnp.where(width == 0, far, other), jnp.where(width == 0, other, far)], axis=2
        )
        chip = jnp.concatenate([own[None], far])
        return jnp.stack([chip, partner(chip, 1, size)]).reshape(rows, features)

    def mlp_hidden(gathered):
        gate_act = dot(gathered, gate_weight[0], last_last)
        up_act = dot(gathered, up_weight[0], last_last)
        return (jax.nn.gelu(gate_act, approximate=True) * up_act).astype(bf16)

    def mlp_sum(part, earlier):
        part = part.reshape(2, size // 2, mine, features)
        chip = scatter_hidden_chip(part, size)
        keep = lax.dynamic_slice_in_dim(chip, width * halves, halves, 2)
        give = lax.dynamic_slice_in_dim(chip, (1 - width) * halves, halves, 2)
        give = give.astype(bf16)
        if earlier is not None:
            give = after(give, earlier)
        row = keep + swap(give, "width").astype(f32)
        return row, keep_bf16(scatter_hidden_z(row, size))

    def encode(acts):
        coder = gather_hidden(acts, size).reshape(rows, halves)
        pre_act = sum_models(dot(coder, enc, plain)).astype(f32) + enc_bias
        latents = jax.nn.softplus(sharpness * pre_act) / sharpness
        return coder, pre_act, latents

    def decode(latents, acts):
        part = dot(latents.astype(bf16), dec, plain).reshape(2, size // 2, mine, halves)
        rebuilt = scatter_hidden_z(scatter_hidden_chip(part, size), size) + dec_bias
        own = 2.0 / tokens * (rebuilt - acts.astype(f32))
        return gather_hidden(keep_bf16(own), size).reshape(rows, halves)

    def back(err, pre_act):
        lat_grad = sum_models(dot(err, dec, last_last)).astype(f32) + sparsity_coef * norm_sum
        return lat_grad * jax.nn.sigmoid(sharpness * pre_act)

    owns = [residual_in[0, c * mine : (c + 1) * mine] for c in range(CHUNKS)]
    fars = [gather_half(own) for own in owns]
    first, dec, squares = lax.optimization_barrier((fars[0], dec, squares))
    fars = [first] + [after(far, enc) for far in fars[1:]]
    gathered = jnp.concatenate([gather_residual(own, far) for own, far in zip(owns, fars)])
    gathered, enc = lax.optimization_barrier((gathered, enc))
    own_square = squares + swap(squares, "width")
    own_norm = jnp.sqrt(own_square + norm_floor)
    norm_sum = own_norm + swap(own_norm, "mp")
    hidden_act = mlp_hidden(gathered)
    parts, part = [], None
    for c in range(CHUNKS):
        act = hidden_act[c * rows : (c + 1) * rows]
        part = dot(act if part is None else after(act, part), down_weight[0], plain)
        parts.append(part)
    acts, row = [], None
    for part in parts:
        row, act = mlp_sum(part, row)
        acts.append(act)
    coded = [encode(a) for a in acts]
    errs = [decode(lat, a) for (_, _, lat), a in zip(coded, acts)]
    grads = [back(err, pre) for err, (_, pre, _) in zip(errs, coded)]

    coder = jnp.concatenate([c for c, _, _ in coded])
    latents = jnp.concatenate([lat for _, _, lat in coded])
    err = jnp.concatenate(errs)
    pre_grad = jnp.concatenate(grads)
    grad_dec_bias = jnp.sum(err.astype(f32), axis=0)
    grad_enc_bias = jnp.sum(pre_grad, axis=0)
    latent_totals = jnp.sum(latents, axis=0)
    grad_dec = dot(latents.astype(bf16), err, first_first)
    grad_dec = grad_dec + sparsity_coef * (latent_totals / own_norm)[:, None] * dec_weight
    grad_enc = dot(coder, pre_grad.astype(bf16), first_first)

    me = lax.axis_index("hidden")
    blocks = latents.reshape(CHUNKS, 2, size // 2, mine, latents.shape[1])
    pieces = []
    for target in range(size):
        source = target ^ me
        piece = lax.dynamic_slice(
            blocks,
            (0, source % 2, source // 2, 0, 0),
            (CHUNKS, 1, 1, mine, latents.shape[1]),
        )
        pieces.append(piece.reshape(CHUNKS * mine, latents.shape[1]))
    latents_out = jnp.concatenate(pieces)
    acts_out = jnp.concatenate(acts)
    return (acts_out[None], latents_out, grad_enc, grad_dec, grad_enc_bias, grad_dec_bias)


def solution(mesh):
    size = mesh.shape["hidden"]

    def step(*args):
        return body(size, *args)

    return jax.shard_map(
        step,
        mesh=mesh,
        in_specs=(
            P("mp", "hidden", None),
            P("mp", ("width", "hidden"), None),
            P("mp", ("width", "hidden"), None),
            P("mp", ("width", "hidden"), None),
            P(("mp", "width"), "hidden"),
            P("hidden"),
            P("hidden", ("mp", "width")),
            P(("mp", "width")),
        ),
        out_specs=(
            P("mp", "hidden", "width"),
            P(None, "hidden"),
            P(("mp", "width"), "hidden"),
            P("hidden", ("mp", "width")),
            P("hidden"),
            P(("mp", "width")),
        ),
        check_vma=False,
    )
```
